32 devices in a mesh: groups: 2 (over x), seq: 8 (over z, y), tensor: 2 (over core).
Axes of the slice: x: 2, y: 2, z: 4, core: 2. Of those that a mesh axis runs over, the one named last changes fastest.
Arguments:
- inputs: bfloat16 [4096, 1536], P(('groups', 'seq'), 'tensor'), parts along dimension 0, may hold values from -6 to 6
- w_dilated: bfloat16 [1536, 3, 1536], P(None, None, 'tensor'), may hold values from -0.09375 to 0.09375
- w_point: bfloat16 [1536, 1536], P(None, 'tensor'), may hold values from -0.15625 to 0.15625
- cotangent: bfloat16 [4096, 1536], P(('groups', 'seq'), 'tensor'), parts along dimension 0, may hold values from -6 to 6
Outputs:
- output: bfloat16 [4096, 1536], P(('groups', 'seq'), 'tensor'), parts along dimension 0
- grad_inputs: bfloat16 [4096, 1536], P(('groups', 'seq'), 'tensor'), parts along dimension 0
- grad_point: float32 [3072, 1536], P(('groups', 'seq'), 'tensor'), parts along dimension 0
The draws below stay inside these ranges and needn't reach their ends.
There are 2 independent parts, one for each index of `groups`. The reference program is written for one: setup_inputs(seed, part) draws one part's arguments, and reference() takes and returns one part's arrays. A program takes and returns all parts, laid end to end along the dimension named above; an argument that names none is the same for every part. Nothing has to cross between parts.
All inputs are finite; a program needn't handle non-finite values.
Results may differ from the reference program's by a relative error of at most 0.007.
Values may be sent and summed in bfloat16 or wider, within the bound.
A program may use at most 64 MiB of HBM per device.

```python
import math
import jax
import jax.numpy as jnp

C = 1536
DILATION_BINS = 32
TOTAL_BINS = 2048
N_TENSOR = 2


def spiked(drawn, own_key, source, target, blocks, factor):
    def block_of(axis_at):
        return (jnp.arange(drawn.shape[axis_at]) // (drawn.shape[axis_at] // blocks)).reshape((-1,) + (1,) * (drawn.ndim - 1 - axis_at))

    one_side = jax.random.permutation(own_key, blocks)[block_of(target)]
    other_side = (block_of(target) + blocks // 2) % blocks
    return jnp.where((block_of(source) == one_side) | (block_of(source) == other_side), factor * drawn, drawn)


def levels(key, dims, shards, low, largest):
    level = 1.0
    for axis_at, blocks in shards:
        heights = jax.random.uniform(jax.random.fold_in(jax.random.fold_in(key, 6), axis_at), (blocks,), jnp.float32, low / len(shards), largest / len(shards))
        level = level * jnp.repeat(jnp.exp(heights), dims[axis_at] // blocks).reshape((-1,) + (1,) * (len(dims) - 1 - axis_at))
    return level


def normal_values(own_key, extent, width, reach, split=(), dtype=jnp.bfloat16):
    values = width * jax.random.normal(own_key, extent, jnp.float32)
    if split:
        values = values * levels(own_key, extent, split, -0.22, 0.18)
    return jnp.clip(values, -reach, reach).astype(dtype)


def gaussian_with(key, shape, scale, reach, shards, heavy, kind=jnp.bfloat16):
    drawn = scale * jax.random.normal(key, shape, jnp.float32)
    if shards:
        drawn = drawn * levels(key, shape, shards, -0.22, 0.18)
    return jnp.clip(spiked(drawn, jax.random.fold_in(key, 3), *heavy), -reach, reach).astype(kind)


def setup_inputs(seed: int = 0, part: int = 0) -> dict:
    seeds = jax.random.split(jax.random.key(seed), 5)
    part_keys = jax.random.split(jax.random.fold_in(seeds[4], part), 5)
    inputs = gaussian_with(part_keys[0], (TOTAL_BINS, C), 1.0, 6.0, ((0, 8), (1, 2)), (0, 1, 8, 2.0))
    w_dilated = normal_values(seeds[1], (C, 3, C), (3 * C) ** -0.5, 0.09375, ((2, 2),))
    w_point = normal_values(seeds[2], (C, C), C ** -0.5, 0.15625, ((1, 2),))
    cotangent = gaussian_with(part_keys[3], (TOTAL_BINS, C), 1.0, 6.0, ((0, 8), (1, 2)), (0, 1, 8, 2.0))
    return {"inputs": inputs, "w_dilated": w_dilated, "w_point": w_point, "cotangent": cotangent}


gelu_cubic = 0.044715
gelu_scale = math.sqrt(2.0 / math.pi)

def gelu_pair(values):
    inner = gelu_scale * (values + gelu_cubic * values * values * values)
    tangent = jnp.tanh(inner)
    result = 0.5 * values * (1.0 + tangent)
    derivative = 0.5 * (1.0 + tangent) + 0.5 * values * (1.0 - tangent * tangent) * gelu_scale * (1.0 + 3.0 * gelu_cubic * values * values)
    return (result, derivative)

def reference(inputs, w_dilated, w_point, cotangent):
    length_bins = inputs.shape[0]
    group_width = C // N_TENSOR
    padded_input = jnp.pad(inputs, ((DILATION_BINS, DILATION_BINS), (0, 0)))
    displaced_rows = [padded_input[kernel_tap_index * DILATION_BINS:kernel_tap_index * DILATION_BINS + length_bins] for kernel_tap_index in range(3)]
    hidden = jnp.dot(displaced_rows[0], w_dilated[:, 0, :], preferred_element_type=jnp.float32)
    hidden = hidden + jnp.dot(displaced_rows[1], w_dilated[:, 1, :], preferred_element_type=jnp.float32)
    hidden = hidden + jnp.dot(displaced_rows[2], w_dilated[:, 2, :], preferred_element_type=jnp.float32)
    activation, derivative = gelu_pair(hidden)
    activation = activation.astype(jnp.bfloat16)
    mixed_sum = inputs.astype(jnp.float32)
    for group_index in range(N_TENSOR):
        lower = group_index * group_width
        part_sum = jnp.dot(activation[:, lower:lower + group_width], w_point[:, lower:lower + group_width].T, preferred_element_type=jnp.float32)
        mixed_sum = mixed_sum + part_sum.astype(jnp.bfloat16).astype(jnp.float32)
    output = mixed_sum.astype(jnp.bfloat16)
    grad_act = jnp.dot(cotangent, w_point, preferred_element_type=jnp.float32)
    hidden_gradient = (grad_act * derivative).astype(jnp.bfloat16)
    grad_point = jnp.dot(cotangent.T, activation, preferred_element_type=jnp.float32)
    padded_gradient = jnp.pad(hidden_gradient, ((DILATION_BINS, DILATION_BINS), (0, 0)))
    back_sum = cotangent.astype(jnp.float32)
    for group_index in range(N_TENSOR):
        lower = group_index * group_width
        part_sum = jnp.zeros((length_bins, C), jnp.float32)
        for kernel_tap_index in range(3):
            anchor_position = (2 - kernel_tap_index) * DILATION_BINS
            part_sum = part_sum + jnp.dot(padded_gradient[anchor_position:anchor_position + length_bins, lower:lower + group_width], w_dilated[:, kernel_tap_index, lower:lower + group_width].T, preferred_element_type=jnp.float32)
        back_sum = back_sum + part_sum.astype(jnp.bfloat16).astype(jnp.float32)
    grad_inputs = back_sum.astype(jnp.bfloat16)
    return (output, grad_inputs, grad_point)
```

```python
import functools
import math

import jax
import jax.numpy as jnp
from jax import lax
from jax.experimental import pallas as pl
from jax.experimental.pallas import tpu as pltpu
from jax.sharding import PartitionSpec as P

DILATION_BINS = 32
MESH = pl.DeviceIdType.MESH

gelu_cubic = 0.044715
gelu_scale = math.sqrt(2.0 / math.pi)


def gelu_pair(values):
    square = values * values
    tangent = jnp.tanh(gelu_scale * (values + gelu_cubic * square * values))
    half = 0.5 * (1.0 + tangent)
    slope = half + 0.5 * values * (1.0 - tangent * tangent) * gelu_scale * (
        1.0 + 3.0 * gelu_cubic * square
    )
    return values * half, slope


def dot_nn(a, b):
    return jnp.dot(a, b, preferred_element_type=jnp.float32)


def dot_nt(a, b):
    return lax.dot_general(a, b, (((1,), (1,)), ((), ())), preferred_element_type=jnp.float32)


def kernel(n, tile, with_point, *refs):
    x_ref, w_hbm, p_hbm, d_ref = refs[:4]
    if with_point:
        out_ref, gi_ref, gp_ref = refs[4:7]
        act, dfull = refs[7:9]
        rest = refs[9:]
    else:
        out_ref, gi_ref, act, dfull = refs[4:8]
        rest = refs[8:]
    (w, p, xfull, slope, ghpad, msend, mrecv, bsend, brecv) = rest[:9]
    (lsem, ssem, rsem, xs_sem, xr_sem, gs_sem, gr_sem) = rest[9:16]
    if with_point:
        (actp, dp, dps, cot_t, gps, gpr, as_sem, ar_sem, ps_sem, pr_sem) = rest[16:]

    s = lax.axis_index("seq")
    t = lax.axis_index("tensor")
    o = 1 - t
    T, H = x_ref.shape
    C = 2 * H
    R = DILATION_BINS
    tiles = H // tile
    bf16 = jnp.bfloat16
    has_low = s > 0
    has_high = s < n - 1
    mine = pl.ds(pl.multiple_of(t * H, H), H)
    other = pl.ds(pl.multiple_of(o * H, H), H)
    nz = n // 2
    z = s // 2
    y = lax.rem(s, 2)
    pair = s + 1 - 2 * y

    def remote(src, dst, send, recv, seq, tensor):
        return pltpu.make_async_remote_copy(
            src_ref=src,
            dst_ref=dst,
            send_sem=send,
            recv_sem=recv,
            device_id={"seq": seq, "tensor": tensor},
            device_id_type=MESH,
        )

    def cols(j):
        return pl.ds(pl.multiple_of(j * tile, tile), tile)

    w_loads = [pltpu.make_async_copy(w_hbm.at[k], w.at[k], lsem.at[k]) for k in range(3)]
    p_load = pltpu.make_async_copy(p_hbm, p, lsem.at[3])
    for load in w_loads:
        load.start()
    p_load.start()

    barrier = pltpu.get_barrier_semaphore()

    def greet(seq, tensor):
        pl.semaphore_signal(
            barrier, inc=1, device_id={"seq": seq, "tensor": tensor}, device_id_type=MESH
        )

    greet(s, o)

    @pl.when(has_low)
    def _():
        greet(s - 1, t)
        greet(s - 1, o)

    @pl.when(has_high)
    def _():
        greet(s + 1, t)
        greet(s + 1, o)

    if with_point:
        for d in range(1, nz):
            greet(lax.rem(z + d, nz) * 2 + y, t)
    xfull[pl.ds(R, T), mine] = x_ref[...]
    dfull[:, mine] = d_ref[...]
    sides = lax.div(s + n - 1, n) + lax.div(2 * n - 2 - s, n)
    pl.semaphore_wait(barrier, 1 + (nz - 1 if with_point else 0) + 2 * sides)

    def to_low(slot, tensor):
        return remote(
            x_ref.at[pl.ds(0, R), :], xfull.at[pl.ds(R + T, R), mine],
            xs_sem.at[slot], xr_sem.at[2 + t], s - 1, tensor,
        )

    def to_high(slot, tensor):
        return remote(
            x_ref.at[pl.ds(T - R, R), :], xfull.at[pl.ds(0, R), mine],
            xs_sem.at[2 + slot], xr_sem.at[t], s + 1, tensor,
        )

    @pl.when(has_low)
    def _():
        to_low(0, t).start()
        to_low(1, o).start()

    @pl.when(has_high)
    def _():
        to_high(0, t).start()
        to_high(1, o).start()

    x_side = remote(x_ref, xfull.at[pl.ds(R, T), mine], ssem.at[0], rsem.at[0], s, o)
    x_side.start()
    d_side = remote(d_ref, dfull.at[:, mine], ssem.at[1], rsem.at[1], s, o)
    d_side.start()
    if with_point:
        d_pair = remote(d_ref, dp, ssem.at[2], rsem.at[2], pair, t)
        d_pair.start()
        d_next = remote(dp, dps, ssem.at[3], rsem.at[3], s, o)
        cot_t[mine, pl.ds(0, T)] = d_ref[...].T

    @pl.when(s == 0)
    def _():
        xfull[pl.ds(0, R), :] = jnp.zeros((R, C), bf16)
        ghpad[pl.ds(0, R), :] = jnp.zeros((R, H), bf16)

    @pl.when(s == n - 1)
    def _():
        xfull[pl.ds(R + T, R), :] = jnp.zeros((R, C), bf16)
        ghpad[pl.ds(R + T, R), :] = jnp.zeros((R, H), bf16)

    remote(x_ref, xfull.at[pl.ds(R, T), other], ssem.at[0], rsem.at[0], s, o).wait_recv()

    @pl.when(has_low)
    def _():
        for half in range(2):
            remote(
                x_ref.at[pl.ds(0, R), :], xfull.at[pl.ds(0, R), pl.ds(half * H, H)],
                xs_sem.at[0], xr_sem.at[half], s - 1, t,
            ).wait_recv()

    @pl.when(has_high)
    def _():
        for half in range(2):
            remote(
                x_ref.at[pl.ds(0, R), :], xfull.at[pl.ds(R + T, R), pl.ds(half * H, H)],
                xs_sem.at[0], xr_sem.at[2 + half], s + 1, t,
            ).wait_recv()

    for load in w_loads:
        load.wait()

    def act_copy(j):
        return remote(
            act.at[j], actp.at[j], as_sem.at[j], ar_sem.at[j], pair, t
        )

    @pl.loop(0, tiles)
    def _(j):
        hidden = dot_nn(xfull[pl.ds(0, T), :], w[0, :, cols(j)])
        hidden += dot_nn(xfull[pl.ds(R, T), :], w[1, :, cols(j)])
        hidden += dot_nn(xfull[pl.ds(2 * R, T), :], w[2, :, cols(j)])
        value, derivative = gelu_pair(hidden)
        act[j] = value.astype(bf16)
        slope[:, cols(j)] = derivative
        if with_point:
            act_copy(j).start()

    if with_point:
        remote(d_ref, dp, ssem.at[2], rsem.at[2], pair, t).wait_recv()
        d_next.start()
        cot_t[mine, pl.ds(T, T)] = dp[...].T
    remote(d_ref, dfull.at[:, other], ssem.at[1], rsem.at[1], s, o).wait_recv()
    p_load.wait()
    if with_point:
        cot_t[other, pl.ds(0, T)] = dfull[:, other].T

    @pl.loop(0, tiles)
    def _(j):
        grad = dot_nn(dfull[...], p[:, cols(j)]) * slope[:, cols(j)]
        ghpad[pl.ds(R, T), cols(j)] = grad.astype(bf16)

    gh_low = remote(
        ghpad.at[pl.ds(R, R), :], ghpad.at[pl.ds(R + T, R), :],
        gs_sem.at[0], gr_sem.at[1], s - 1, t,
    )
    gh_high = remote(
        ghpad.at[pl.ds(T, R), :], ghpad.at[pl.ds(0, R), :],
        gs_sem.at[1], gr_sem.at[0], s + 1, t,
    )

    @pl.when(has_low)
    def _():
        gh_low.start()

    @pl.when(has_high)
    def _():
        gh_high.start()

    def point_copy(d, j):
        return remote(
            gps.at[d - 1, j], gpr.at[d - 1, j], ps_sem.at[d - 1, j], pr_sem.at[d - 1, j],
            lax.rem(z + d, nz) * 2 + y, t,
        )

    if with_point:
        rows = gp_ref.shape[0]
        remote(dp, dps, ssem.at[3], rsem.at[3], s, o).wait_recv()
        cot_t[other, pl.ds(T, T)] = dps[...].T

        @pl.loop(0, tiles)
        def _(j):
            act_copy(j).wait_recv()

            def block(d):
                owner = lax.rem(z + d, nz) * 2 + y
                at = pl.ds(pl.multiple_of(owner * rows, rows), rows)
                return dot_nn(cot_t[at, pl.ds(0, T)], act[j]) + dot_nn(
                    cot_t[at, pl.ds(T, T)], actp[j]
                )

            for d in range(1, nz):
                gps[d - 1, j] = block(d).astype(bf16)
                point_copy(d, j).start()
            gp_ref[:, cols(j)] = block(0)

    def mixed(at):
        total = dot_nt(act[0], p[at, pl.ds(0, tile)])
        for i in range(1, tiles):
            total += dot_nt(act[i], p[at, pl.ds(i * tile, tile)])
        return total.astype(bf16)

    @pl.loop(0, tiles)
    def _(j):
        msend[:, cols(j)] = mixed(pl.ds(pl.multiple_of(o * H + j * tile, tile), tile))

    m_side = remote(msend, mrecv, ssem.at[4], rsem.at[4], s, o)
    m_side.start()

    @pl.when(has_low)
    def _():
        remote(
            ghpad.at[pl.ds(R, R), :], ghpad.at[pl.ds(0, R), :],
            gs_sem.at[0], gr_sem.at[0], s - 1, t,
        ).wait_recv()

    @pl.when(has_high)
    def _():
        remote(
            ghpad.at[pl.ds(R, R), :], ghpad.at[pl.ds(R + T, R), :],
            gs_sem.at[0], gr_sem.at[1], s + 1, t,
        ).wait_recv()

    def back(at):
        total = dot_nt(ghpad[pl.ds(2 * R, T), :], w[0, at, :])
        total += dot_nt(ghpad[pl.ds(R, T), :], w[1, at, :])
        total += dot_nt(ghpad[pl.ds(0, T), :], w[2, at, :])
        return total.astype(bf16)

    @pl.loop(0, tiles)
    def _(j):
        bsend[:, cols(j)] = back(pl.ds(pl.multiple_of(o * H + j * tile, tile), tile))

    b_side = remote(bsend, brecv, ssem.at[5], rsem.at[5], s, o)
    b_side.start()
    m_side.wait_recv()

    @pl.loop(0, tiles)
    def _(j):
        own = mixed(pl.ds(pl.multiple_of(t * H + j * tile, tile), tile))
        total = x_ref[:, cols(j)].astype(jnp.float32) + own.astype(jnp.float32)
        out_ref[:, cols(j)] = (total + mrecv[:, cols(j)].astype(jnp.float32)).astype(bf16)

    b_side.wait_recv()

    @pl.loop(0, tiles)
    def _(j):
        own = back(pl.ds(pl.multiple_of(t * H + j * tile, tile), tile))
        total = d_ref[:, cols(j)].astype(jnp.float32) + own.astype(jnp.float32)
        gi_ref[:, cols(j)] = (total + brecv[:, cols(j)].astype(jnp.float32)).astype(bf16)

    if with_point:

        @pl.loop(0, tiles)
        def _(j):
            total = gp_ref[:, cols(j)]
            for d in range(1, nz):
                point_copy(d, j).wait_recv()
                total += gpr[d - 1, j].astype(jnp.float32)
            gp_ref[:, cols(j)] = total

    @pl.when(has_low)
    def _():
        to_low(0, t).wait_send()
        to_low(1, o).wait_send()
        gh_low.wait_send()

    @pl.when(has_high)
    def _():
        to_high(0, t).wait_send()
        to_high(1, o).wait_send()
        gh_high.wait_send()

    x_side.wait_send()
    d_side.wait_send()
    m_side.wait_send()
    b_side.wait_send()
    if with_point:
        d_pair.wait_send()
        d_next.wait_send()

        @pl.loop(0, tiles)
        def _(j):
            act_copy(j).wait_send()
            for d in range(1, nz):
                point_copy(d, j).wait_send()


def local(n, inputs, w_dilated, w_point, cotangent):
    T, H = inputs.shape
    C = w_point.shape[0]
    R = DILATION_BINS
    tile = 256
    tiles = H // tile
    rows = C // n
    bf16, f32 = jnp.bfloat16, jnp.float32
    with_point = rows % 16 == 0 and n % 2 == 0
    nz = n // 2
    vmem = pl.BlockSpec(memory_space=pltpu.VMEM)
    hbm = pl.BlockSpec(memory_space=pl.ANY)
    plane = jax.ShapeDtypeStruct((T, H), bf16)
    act_shape = (tiles, T, tile)
    outs = [plane, plane]
    scratch = []
    if with_point:
        outs += [jax.ShapeDtypeStruct((rows, H), f32)]
        scratch += [pltpu.VMEM(act_shape, bf16), pltpu.VMEM((T, C), bf16)]
    else:
        outs += [jax.ShapeDtypeStruct(act_shape, bf16), jax.ShapeDtypeStruct((T, C), bf16)]
    dma = pltpu.SemaphoreType.DMA
    scratch += [
        pltpu.VMEM((3, C, H), bf16),
        pltpu.VMEM((C, H), bf16),
        pltpu.VMEM((T + 2 * R, C), bf16),
        pltpu.VMEM((T, H), f32),
        pltpu.VMEM((T + 2 * R, H), bf16),
        pltpu.VMEM((T, H), bf16),
        pltpu.VMEM((T, H), bf16),
        pltpu.VMEM((T, H), bf16),
        pltpu.VMEM((T, H), bf16),
        dma((4,)), dma((6,)), dma((6,)), dma((4,)), dma((4,)), dma((2,)), dma((2,)),
    ]
    if with_point:
        scratch += [
            pltpu.VMEM(act_shape, bf16),
            pltpu.VMEM((T, H), bf16),
            pltpu.VMEM((T, H), bf16),
            pltpu.VMEM((C, 2 * T), bf16),
            pltpu.VMEM((nz - 1, tiles, rows, tile), bf16),
            pltpu.VMEM((nz - 1, tiles, rows, tile), bf16),
            dma((tiles,)), dma((tiles,)), dma((nz - 1, tiles)), dma((nz - 1, tiles)),
        ]
    results = pl.pallas_call(
        functools.partial(kernel, n, tile, with_point),
        out_shape=outs,
        in_specs=[vmem, hbm, hbm, vmem],
        out_specs=[vmem] * len(outs),
        scratch_shapes=scratch,
        compiler_params=pltpu.CompilerParams(
            collective_id=0, has_side_effects=True, vmem_limit_bytes=48 * 1024 * 1024
        ),
    )(inputs, jnp.transpose(w_dilated, (1, 0, 2)), w_point, cotangent)
    if with_point:
        return tuple(results)
    output, grad_inputs, act, full_grad = results
    activation = jnp.transpose(act, (1, 0, 2)).reshape(T, H)
    grad_point = lax.psum_scatter(
        jnp.einsum("to,tc->oc", full_grad, activation, preferred_element_type=f32),
        "seq",
        scatter_dimension=0,
        tiled=True,
    )
    return (output, grad_inputs, grad_point)


def solution(mesh):
    placed = (
        P(("groups", "seq"), "tensor"),
        P(None, None, "tensor"),
        P(None, "tensor"),
        P(("groups", "seq"), "tensor"),
    )
    return jax.shard_map(
        functools.partial(local, mesh.shape["seq"]),
        mesh=mesh,
        in_specs=placed,
        out_specs=(
            P(("groups", "seq"), "tensor"),
            P(("groups", "seq"), "tensor"),
            P(("groups", "seq"), "tensor"),
        ),
        check_vma=False,
    )
```

```python
import functools
import math

import jax
import jax.numpy as jnp
from jax import lax
from jax.experimental import pallas as pl
from jax.experimental.pallas import tpu as pltpu
from jax.sharding import PartitionSpec as P

DILATION_BINS = 32
MESH = pl.DeviceIdType.MESH

gelu_cubic = 0.044715
gelu_scale = math.sqrt(2.0 / math.pi)


def gelu_pair(values):
    square = values * values
    tangent = jnp.tanh(gelu_scale * (values + gelu_cubic * square * values))
    half = 0.5 * (1.0 + tangent)
    slope = half + 0.5 * values * (1.0 - tangent * tangent) * gelu_scale * (
        1.0 + 3.0 * gelu_cubic * square
    )
    return values * half, slope


def dot_nn(a, b):
    return jnp.dot(a, b, preferred_element_type=jnp.float32)


def dot_nt(a, b):
    return lax.dot_general(a, b, (((1,), (1,)), ((), ())), preferred_element_type=jnp.float32)


def kernel(n, tile, with_point, *refs):
    x_hbm, w_hbm, p_hbm, d_hbm = refs[:4]
    if with_point:
        out_ref, gi_ref, gp_ref = refs[4:7]
        act, dfull = refs[7:9]
        rest = refs[9:]
    else:
        out_ref, gi_ref, act, dfull = refs[4:8]
        rest = refs[8:]
    (w, p, xfull, slope, ghpad, msend, mrecv, bsend, brecv) = rest[:9]
    (lsem, ssem, rsem, xs_sem, xr_sem, gs_sem, gr_sem) = rest[9:16]
    if with_point:
        (actp, dp, dps, cot_t, gps, gpr, as_sem, ar_sem, ps_sem, pr_sem) = rest[16:]

    s = lax.axis_index("seq")
    t = lax.axis_index("tensor")
    o = 1 - t
    T, H = x_hbm.shape
    C = 2 * H
    R = DILATION_BINS
    tiles = H // tile
    bf16 = jnp.bfloat16
    has_low = s > 0
    has_high = s < n - 1
    mine = pl.ds(pl.multiple_of(t * H, H), H)
    other = pl.ds(pl.multiple_of(o * H, H), H)
    nz = n // 2
    z = s // 2
    y = lax.rem(s, 2)
    pair = s + 1 - 2 * y

    def remote(src, dst, send, recv, seq, tensor):
        return pltpu.make_async_remote_copy(
            src_ref=src,
            dst_ref=dst,
            send_sem=send,
            recv_sem=recv,
            device_id={"seq": seq, "tensor": tensor},
            device_id_type=MESH,
        )

    def cols(j):
        return pl.ds(pl.multiple_of(j * tile, tile), tile)

    x_ref = xfull.at[pl.ds(R, T), mine]
    d_ref = dfull.at[:, mine]
    x_load = pltpu.make_async_copy(x_hbm, x_ref, lsem.at[0])
    d_load = pltpu.make_async_copy(d_hbm, d_ref, lsem.at[1])
    p_load = pltpu.make_async_copy(p_hbm, p, lsem.at[2])
    x_load.start()
    d_load.start()

    def w_load(j):
        return pltpu.make_async_copy(
            w_hbm.at[:, :, cols(j)], w.at[:, :, cols(j)], lsem.at[3 + j]
        )

    for j in range(tiles):
        w_load(j).start()
    p_load.start()

    barrier = pltpu.get_barrier_semaphore()

    def greet(seq, tensor):
        pl.semaphore_signal(
            barrier, inc=1, device_id={"seq": seq, "tensor": tensor}, device_id_type=MESH
        )

    greet(s, o)

    @pl.when(has_low)
    def _():
        greet(s - 1, t)
        greet(s - 1, o)

    @pl.when(has_high)
    def _():
        greet(s + 1, t)
        greet(s + 1, o)

    if with_point:
        for d in range(1, nz):
            greet(lax.rem(z + d, nz) * 2 + y, t)
    sides = lax.div(s + n - 1, n) + lax.div(2 * n - 2 - s, n)
    pl.semaphore_wait(barrier, 1 + (nz - 1 if with_point else 0) + 2 * sides)

    def to_low(slot, tensor):
        return remote(
            x_hbm.at[pl.ds(0, R), :], xfull.at[pl.ds(R + T, R), mine],
            xs_sem.at[slot], xr_sem.at[2 + t], s - 1, tensor,
        )

    def to_high(slot, tensor):
        return remote(
            x_hbm.at[pl.ds(T - R, R), :], xfull.at[pl.ds(0, R), mine],
            xs_sem.at[2 + slot], xr_sem.at[t], s + 1, tensor,
        )

    @pl.when(has_low)
    def _():
        to_low(0, t).start()
        to_low(1, o).start()

    @pl.when(has_high)
    def _():
        to_high(0, t).start()
        to_high(1, o).start()

    x_side = remote(x_hbm, xfull.at[pl.ds(R, T), mine], ssem.at[0], rsem.at[0], s, o)
    x_side.start()
    d_side = remote(d_hbm, dfull.at[:, mine], ssem.at[1], rsem.at[1], s, o)
    d_side.start()
    if with_point:
        d_pair = remote(d_hbm, dp, ssem.at[2], rsem.at[2], pair, t)
        d_pair.start()
        d_next = remote(dp, dps, ssem.at[3], rsem.at[3], s, o)
        d_load.wait()
        cot_t[mine, pl.ds(0, T)] = d_ref[...].T
    else:
        d_load.wait()

    @pl.when(s == 0)
    def _():
        xfull[pl.ds(0, R), :] = jnp.zeros((R, C), bf16)
        ghpad[pl.ds(0, R), :] = jnp.zeros((R, H), bf16)

    @pl.when(s == n - 1)
    def _():
        xfull[pl.ds(R + T, R), :] = jnp.zeros((R, C), bf16)
        ghpad[pl.ds(R + T, R), :] = jnp.zeros((R, H), bf16)

    remote(x_hbm, xfull.at[pl.ds(R, T), other], ssem.at[0], rsem.at[0], s, o).wait_recv()

    @pl.when(has_low)
    def _():
        for half in range(2):
            remote(
                x_hbm.at[pl.ds(0, R), :], xfull.at[pl.ds(0, R), pl.ds(half * H, H)],
                xs_sem.at[0], xr_sem.at[half], s - 1, t,
            ).wait_recv()

    @pl.when(has_high)
    def _():
        for half in range(2):
            remote(
                x_hbm.at[pl.ds(0, R), :], xfull.at[pl.ds(R + T, R), pl.ds(half * H, H)],
                xs_sem.at[0], xr_sem.at[2 + half], s + 1, t,
            ).wait_recv()

    x_load.wait()

    def act_copy(j):
        return remote(
            act.at[j], actp.at[j], as_sem.at[j], ar_sem.at[j], pair, t
        )

    @pl.loop(0, tiles)
    def _(j):
        w_load(j).wait()
        hidden = dot_nn(xfull[pl.ds(0, T), :], w[0, :, cols(j)])
        hidden += dot_nn(xfull[pl.ds(R, T), :], w[1, :, cols(j)])
        hidden += dot_nn(xfull[pl.ds(2 * R, T), :], w[2, :, cols(j)])
        value, derivative = gelu_pair(hidden)
        act[j] = value.astype(bf16)
        slope[:, cols(j)] = derivative
        if with_point:
            act_copy(j).start()

    if with_point:
        remote(d_hbm, dp, ssem.at[2], rsem.at[2], pair, t).wait_recv()
        d_next.start()
        cot_t[mine, pl.ds(T, T)] = dp[...].T
    remote(d_hbm, dfull.at[:, other], ssem.at[1], rsem.at[1], s, o).wait_recv()
    p_load.wait()
    if with_point:
        cot_t[other, pl.ds(0, T)] = dfull[:, other].T

    @pl.loop(0, tiles)
    def _(j):
        grad = dot_nn(dfull[...], p[:, cols(j)]) * slope[:, cols(j)]
        ghpad[pl.ds(R, T), cols(j)] = grad.astype(bf16)

    gh_low = remote(
        ghpad.at[pl.ds(R, R), :], ghpad.at[pl.ds(R + T, R), :],
        gs_sem.at[0], gr_sem.at[1], s - 1, t,
    )
    gh_high = remote(
        ghpad.at[pl.ds(T, R), :], ghpad.at[pl.ds(0, R), :],
        gs_sem.at[1], gr_sem.at[0], s + 1, t,
    )

    @pl.when(has_low)
    def _():
        gh_low.start()

    @pl.when(has_high)
    def _():
        gh_high.start()

    def point_copy(d, j):
        return remote(
            gps.at[d - 1, j], gpr.at[d - 1, j], ps_sem.at[d - 1, j], pr_sem.at[d - 1, j],
            lax.rem(z + d, nz) * 2 + y, t,
        )

    if with_point:
        rows = gp_ref.shape[0]
        remote(dp, dps, ssem.at[3], rsem.at[3], s, o).wait_recv()
        cot_t[other, pl.ds(T, T)] = dps[...].T

        @pl.loop(0, tiles)
        def _(j):
            act_copy(j).wait_recv()

            def block(d):
                owner = lax.rem(z + d, nz) * 2 + y
                at = pl.ds(pl.multiple_of(owner * rows, rows), rows)
                return dot_nn(cot_t[at, pl.ds(0, T)], act[j]) + dot_nn(
                    cot_t[at, pl.ds(T, T)], actp[j]
                )

            for d in range(1, nz):
                gps[d - 1, j] = block(d).astype(bf16)
                point_copy(d, j).start()
            gp_ref[:, cols(j)] = block(0)

    def mixed(at):
        total = dot_nt(act[0], p[at, pl.ds(0, tile)])
        for i in range(1, tiles):
            total += dot_nt(act[i], p[at, pl.ds(i * tile, tile)])
        return total.astype(bf16)

    @pl.loop(0, tiles)
    def _(j):
        msend[:, cols(j)] = mixed(pl.ds(pl.multiple_of(o * H + j * tile, tile), tile))

    m_side = remote(msend, mrecv, ssem.at[4], rsem.at[4], s, o)
    m_side.start()

    @pl.when(has_low)
    def _():
        remote(
            ghpad.at[pl.ds(R, R), :], ghpad.at[pl.ds(0, R), :],
            gs_sem.at[0], gr_sem.at[0], s - 1, t,
        ).wait_recv()

    @pl.when(has_high)
    def _():
        remote(
            ghpad.at[pl.ds(R, R), :], ghpad.at[pl.ds(R + T, R), :],
            gs_sem.at[0], gr_sem.at[1], s + 1, t,
        ).wait_recv()

    def back(at):
        total = dot_nt(ghpad[pl.ds(2 * R, T), :], w[0, at, :])
        total += dot_nt(ghpad[pl.ds(R, T), :], w[1, at, :])
        total += dot_nt(ghpad[pl.ds(0, T), :], w[2, at, :])
        return total.astype(bf16)

    @pl.loop(0, tiles)
    def _(j):
        bsend[:, cols(j)] = back(pl.ds(pl.multiple_of(o * H + j * tile, tile), tile))

    b_side = remote(bsend, brecv, ssem.at[5], rsem.at[5], s, o)
    b_side.start()
    m_side.wait_recv()

    @pl.loop(0, tiles)
    def _(j):
        own = mixed(pl.ds(pl.multiple_of(t * H + j * tile, tile), tile))
        total = x_ref[:, cols(j)].astype(jnp.float32) + own.astype(jnp.float32)
        out_ref[:, cols(j)] = (total + mrecv[:, cols(j)].astype(jnp.float32)).astype(bf16)

    b_side.wait_recv()

    @pl.loop(0, tiles)
    def _(j):
        own = back(pl.ds(pl.multiple_of(t * H + j * tile, tile), tile))
        total = d_ref[:, cols(j)].astype(jnp.float32) + own.astype(jnp.float32)
        gi_ref[:, cols(j)] = (total + brecv[:, cols(j)].astype(jnp.float32)).astype(bf16)

    if with_point:

        @pl.loop(0, tiles)
        def _(j):
            total = gp_ref[:, cols(j)]
            for d in range(1, nz):
                point_copy(d, j).wait_recv()
                total += gpr[d - 1, j].astype(jnp.float32)
            gp_ref[:, cols(j)] = total

    @pl.when(has_low)
    def _():
        to_low(0, t).wait_send()
        to_low(1, o).wait_send()
        gh_low.wait_send()

    @pl.when(has_high)
    def _():
        to_high(0, t).wait_send()
        to_high(1, o).wait_send()
        gh_high.wait_send()

    x_side.wait_send()
    d_side.wait_send()
    m_side.wait_send()
    b_side.wait_send()
    if with_point:
        d_pair.wait_send()
        d_next.wait_send()

        @pl.loop(0, tiles)
        def _(j):
            act_copy(j).wait_send()
            for d in range(1, nz):
                point_copy(d, j).wait_send()


def local(n, inputs, w_dilated, w_point, cotangent):
    T, H = inputs.shape
    C = w_point.shape[0]
    R = DILATION_BINS
    tile = 256
    tiles = H // tile
    rows = C // n
    bf16, f32 = jnp.bfloat16, jnp.float32
    with_point = rows % 16 == 0 and n % 2 == 0
    nz = n // 2
    vmem = pl.BlockSpec(memory_space=pltpu.VMEM)
    hbm = pl.BlockSpec(memory_space=pltpu.HBM)
    plane = jax.ShapeDtypeStruct((T, H), bf16)
    act_shape = (tiles, T, tile)
    outs = [plane, plane]
    scratch = []
    if with_point:
        outs += [jax.ShapeDtypeStruct((rows, H), f32)]
        scratch += [pltpu.VMEM(act_shape, bf16), pltpu.VMEM((T, C), bf16)]
    else:
        outs += [jax.ShapeDtypeStruct(act_shape, bf16), jax.ShapeDtypeStruct((T, C), bf16)]
    dma = pltpu.SemaphoreType.DMA
    scratch += [
        pltpu.VMEM((3, C, H), bf16),
        pltpu.VMEM((C, H), bf16),
        pltpu.VMEM((T + 2 * R, C), bf16),
        pltpu.VMEM((T, H), f32),
        pltpu.VMEM((T + 2 * R, H), bf16),
        pltpu.VMEM((T, H), bf16),
        pltpu.VMEM((T, H), bf16),
        pltpu.VMEM((T, H), bf16),
        pltpu.VMEM((T, H), bf16),
        dma((3 + tiles,)), dma((6,)), dma((6,)), dma((4,)), dma((4,)), dma((2,)), dma((2,)),
    ]
    if with_point:
        scratch += [
            pltpu.VMEM(act_shape, bf16),
            pltpu.VMEM((T, H), bf16),
            pltpu.VMEM((T, H), bf16),
            pltpu.VMEM((C, 2 * T), bf16),
            pltpu.VMEM((nz - 1, tiles, rows, tile), bf16),
            pltpu.VMEM((nz - 1, tiles, rows, tile), bf16),
            dma((tiles,)), dma((tiles,)), dma((nz - 1, tiles)), dma((nz - 1, tiles)),
        ]
    results = pl.pallas_call(
        functools.partial(kernel, n, tile, with_point),
        out_shape=outs,
        in_specs=[hbm] * 4,
        out_specs=[vmem] * len(outs),
        scratch_shapes=scratch,
        compiler_params=pltpu.CompilerParams(
            collective_id=0, has_side_effects=True, vmem_limit_bytes=60 * 1024 * 1024
        ),
    )(inputs, jnp.transpose(w_dilated, (1, 0, 2)), w_point, cotangent)
    if with_point:
        return tuple(results)
    output, grad_inputs, act, full_grad = results
    activation = jnp.transpose(act, (1, 0, 2)).reshape(T, H)
    grad_point = lax.psum_scatter(
        jnp.einsum("to,tc->oc", full_grad, activation, preferred_element_type=f32),
        "seq",
        scatter_dimension=0,
        tiled=True,
    )
    return (output, grad_inputs, grad_point)


def solution(mesh):
    placed = (
        P(("groups", "seq"), "tensor"),
        P(None, None, "tensor"),
        P(None, "tensor"),
        P(("groups", "seq"), "tensor"),
    )
    return jax.shard_map(
        functools.partial(local, mesh.shape["seq"]),
        mesh=mesh,
        in_specs=placed,
        out_specs=(
            P(("groups", "seq"), "tensor"),
            P(("groups", "seq"), "tensor"),
            P(("groups", "seq"), "tensor"),
        ),
        check_vma=False,
    )
```

```python
import functools
import math

import jax
import jax.numpy as jnp
from jax import lax
from jax.experimental import pallas as pl
from jax.experimental.pallas import tpu as pltpu
from jax.sharding import PartitionSpec as P

DILATION_BINS = 32
MESH = pl.DeviceIdType.MESH

gelu_cubic = 0.044715
gelu_scale = math.sqrt(2.0 / math.pi)


def gelu_pair(values):
    square = values * values
    tangent = jnp.tanh(gelu_scale * (values + gelu_cubic * square * values))
    half = 0.5 * (1.0 + tangent)
    slope = half + 0.5 * values * (1.0 - tangent * tangent) * gelu_scale * (
        1.0 + 3.0 * gelu_cubic * square
    )
    return values * half, slope


def dot_nn(a, b):
    return jnp.dot(a, b, preferred_element_type=jnp.float32)


def dot_nt(a, b):
    return lax.dot_general(a, b, (((1,), (1,)), ((), ())), preferred_element_type=jnp.float32)


def kernel(n, tile, with_point, *refs):
    x_hbm, w_hbm, p_hbm, d_hbm = refs[:4]
    if with_point:
        out_ref, gi_ref, gp_ref = refs[4:7]
        act, dfull = refs[7:9]
        rest = refs[9:]
    else:
        out_ref, gi_ref, act, dfull = refs[4:8]
        rest = refs[8:]
    (w, p, xfull, slope, ghpad, msend, mrecv, bsend, brecv) = rest[:9]
    (lsem, ssem, rsem, xs_sem, xr_sem, gs_sem, gr_sem) = rest[9:16]
    if with_point:
        (actp, dp, dps, cot_t, gps, gpr, as_sem, ar_sem, ps_sem, pr_sem) = rest[16:]

    s = lax.axis_index("seq")
    t = lax.axis_index("tensor")
    o = 1 - t
    T, H = x_hbm.shape
    C = 2 * H
    R = DILATION_BINS
    tiles = H // tile
    bf16 = jnp.bfloat16
    has_low = s > 0
    has_high = s < n - 1
    mine = pl.ds(pl.multiple_of(t * H, H), H)
    other = pl.ds(pl.multiple_of(o * H, H), H)
    nz = n // 2
    z = s // 2
    y = lax.rem(s, 2)
    pair = s + 1 - 2 * y

    def remote(src, dst, send, recv, seq, tensor):
        return pltpu.make_async_remote_copy(
            src_ref=src,
            dst_ref=dst,
            send_sem=send,
            recv_sem=recv,
            device_id={"seq": seq, "tensor": tensor},
            device_id_type=MESH,
        )

    def cols(j):
        return pl.ds(pl.multiple_of(j * tile, tile), tile)

    x_ref = xfull.at[pl.ds(R, T), mine]
    d_ref = dfull.at[:, mine]
    x_load = pltpu.make_async_copy(x_hbm, x_ref, lsem.at[0])
    d_load = pltpu.make_async_copy(d_hbm, d_ref, lsem.at[1])
    p_load = pltpu.make_async_copy(p_hbm, p, lsem.at[2])
    x_load.start()
    d_load.start()

    def w_load(j):
        return pltpu.make_async_copy(
            w_hbm.at[:, :, cols(j)], w.at[:, :, cols(j)], lsem.at[3 + j]
        )

    for j in range(tiles):
        w_load(j).start()
    p_load.start()

    barrier = pltpu.get_barrier_semaphore()

    def greet(seq, tensor):
        pl.semaphore_signal(
            barrier, inc=1, device_id={"seq": seq, "tensor": tensor}, device_id_type=MESH
        )

    greet(s, o)

    @pl.when(has_low)
    def _():
        greet(s - 1, t)
        greet(s - 1, o)

    @pl.when(has_high)
    def _():
        greet(s + 1, t)
        greet(s + 1, o)

    if with_point:
        for d in range(1, nz):
            greet(lax.rem(z + d, nz) * 2 + y, t)
    sides = lax.div(s + n - 1, n) + lax.div(2 * n - 2 - s, n)
    pl.semaphore_wait(barrier, 1 + (nz - 1 if with_point else 0) + 2 * sides)

    def to_low(slot, tensor):
        return remote(
            x_hbm.at[pl.ds(0, R), :], xfull.at[pl.ds(R + T, R), mine],
            xs_sem.at[slot], xr_sem.at[2 + t], s - 1, tensor,
        )

    def to_high(slot, tensor):
        return remote(
            x_hbm.at[pl.ds(T - R, R), :], xfull.at[pl.ds(0, R), mine],
            xs_sem.at[2 + slot], xr_sem.at[t], s + 1, tensor,
        )

    @pl.when(has_low)
    def _():
        to_low(0, t).start()
        to_low(1, o).start()

    @pl.when(has_high)
    def _():
        to_high(0, t).start()
        to_high(1, o).start()

    x_side = remote(x_hbm, xfull.at[pl.ds(R, T), mine], ssem.at[0], rsem.at[0], s, o)
    x_side.start()
    d_side = remote(d_hbm, dfull.at[:, mine], ssem.at[1], rsem.at[1], s, o)
    d_side.start()
    if with_point:
        d_pair = remote(d_hbm, dp, ssem.at[2], rsem.at[2], pair, t)
        d_pair.start()
        d_next = remote(dp, dps, ssem.at[3], rsem.at[3], s, o)
        d_load.wait()
        cot_t[mine, pl.ds(0, T)] = d_ref[...].T
    else:
        d_load.wait()

    @pl.when(s == 0)
    def _():
        xfull[pl.ds(0, R), :] = jnp.zeros((R, C), bf16)
        ghpad[pl.ds(0, R), :] = jnp.zeros((R, H), bf16)

    @pl.when(s == n - 1)
    def _():
        xfull[pl.ds(R + T, R), :] = jnp.zeros((R, C), bf16)
        ghpad[pl.ds(R + T, R), :] = jnp.zeros((R, H), bf16)

    remote(x_hbm, xfull.at[pl.ds(R, T), other], ssem.at[0], rsem.at[0], s, o).wait_recv()

    @pl.when(has_low)
    def _():
        for half in range(2):
            remote(
                x_hbm.at[pl.ds(0, R), :], xfull.at[pl.ds(0, R), pl.ds(half * H, H)],
                xs_sem.at[0], xr_sem.at[half], s - 1, t,
            ).wait_recv()

    @pl.when(has_high)
    def _():
        for half in range(2):
            remote(
                x_hbm.at[pl.ds(0, R), :], xfull.at[pl.ds(R + T, R), pl.ds(half * H, H)],
                xs_sem.at[0], xr_sem.at[2 + half], s + 1, t,
            ).wait_recv()

    x_load.wait()

    def act_copy(j):
        return remote(
            act.at[j], actp.at[j], as_sem.at[j], ar_sem.at[j], pair, t
        )

    @pl.loop(0, tiles)
    def _(j):
        w_load(j).wait()
        hidden = dot_nn(xfull[pl.ds(0, T), :], w[0, :, cols(j)])
        hidden += dot_nn(xfull[pl.ds(R, T), :], w[1, :, cols(j)])
        hidden += dot_nn(xfull[pl.ds(2 * R, T), :], w[2, :, cols(j)])
        value, derivative = gelu_pair(hidden)
        act[j] = value.astype(bf16)
        slope[:, cols(j)] = derivative
        if with_point:
            act_copy(j).start()

    if with_point:
        remote(d_hbm, dp, ssem.at[2], rsem.at[2], pair, t).wait_recv()
        d_next.start()
        cot_t[mine, pl.ds(T, T)] = dp[...].T
    remote(d_hbm, dfull.at[:, other], ssem.at[1], rsem.at[1], s, o).wait_recv()
    p_load.wait()
    if with_point:
        cot_t[other, pl.ds(0, T)] = dfull[:, other].T

    def point_copy(d, j):
        return remote(
            gps.at[d - 1, j], gpr.at[d - 1, j], ps_sem.at[d - 1, j], pr_sem.at[d - 1, j],
            lax.rem(z + d, nz) * 2 + y, t,
        )

    if with_point:
        rows = gp_ref.shape[0]
        remote(dp, dps, ssem.at[3], rsem.at[3], s, o).wait_recv()
        cot_t[other, pl.ds(T, T)] = dps[...].T

        def block(d, j):
            owner = lax.rem(z + d, nz) * 2 + y
            at = pl.ds(pl.multiple_of(owner * rows, rows), rows)
            return dot_nn(cot_t[at, pl.ds(0, T)], act[j]) + dot_nn(
                cot_t[at, pl.ds(T, T)], actp[j]
            )

        @pl.loop(0, tiles)
        def _(j):
            act_copy(j).wait_recv()

            for d in range(1, nz):
                gps[d - 1, j] = block(d, j).astype(bf16)
                point_copy(d, j).start()

    @pl.loop(0, tiles)
    def _(j):
        grad = dot_nn(dfull[...], p[:, cols(j)]) * slope[:, cols(j)]
        ghpad[pl.ds(R, T), cols(j)] = grad.astype(bf16)

    gh_low = remote(
        ghpad.at[pl.ds(R, R), :], ghpad.at[pl.ds(R + T, R), :],
        gs_sem.at[0], gr_sem.at[1], s - 1, t,
    )
    gh_high = remote(
        ghpad.at[pl.ds(T, R), :], ghpad.at[pl.ds(0, R), :],
        gs_sem.at[1], gr_sem.at[0], s + 1, t,
    )

    @pl.when(has_low)
    def _():
        gh_low.start()

    @pl.when(has_high)
    def _():
        gh_high.start()

    def mixed(at):
        total = dot_nt(act[0], p[at, pl.ds(0, tile)])
        for i in range(1, tiles):
            total += dot_nt(act[i], p[at, pl.ds(i * tile, tile)])
        return total.astype(bf16)

    @pl.loop(0, tiles)
    def _(j):
        msend[:, cols(j)] = mixed(pl.ds(pl.multiple_of(o * H + j * tile, tile), tile))

    m_side = remote(msend, mrecv, ssem.at[4], rsem.at[4], s, o)
    m_side.start()

    @pl.when(has_low)
    def _():
        remote(
            ghpad.at[pl.ds(R, R), :], ghpad.at[pl.ds(0, R), :],
            gs_sem.at[0], gr_sem.at[0], s - 1, t,
        ).wait_recv()

    @pl.when(has_high)
    def _():
        remote(
            ghpad.at[pl.ds(R, R), :], ghpad.at[pl.ds(R + T, R), :],
            gs_sem.at[0], gr_sem.at[1], s + 1, t,
        ).wait_recv()

    def back(at):
        total = dot_nt(ghpad[pl.ds(2 * R, T), :], w[0, at, :])
        total += dot_nt(ghpad[pl.ds(R, T), :], w[1, at, :])
        total += dot_nt(ghpad[pl.ds(0, T), :], w[2, at, :])
        return total.astype(bf16)

    @pl.loop(0, tiles)
    def _(j):
        bsend[:, cols(j)] = back(pl.ds(pl.multiple_of(o * H + j * tile, tile), tile))

    b_side = remote(bsend, brecv, ssem.at[5], rsem.at[5], s, o)
    b_side.start()
    m_side.wait_recv()

    @pl.loop(0, tiles)
    def _(j):
        own = mixed(pl.ds(pl.multiple_of(t * H + j * tile, tile), tile))
        total = x_ref[:, cols(j)].astype(jnp.float32) + own.astype(jnp.float32)
        out_ref[:, cols(j)] = (total + mrecv[:, cols(j)].astype(jnp.float32)).astype(bf16)

    b_side.wait_recv()

    @pl.loop(0, tiles)
    def _(j):
        own = back(pl.ds(pl.multiple_of(t * H + j * tile, tile), tile))
        total = d_ref[:, cols(j)].astype(jnp.float32) + own.astype(jnp.float32)
        gi_ref[:, cols(j)] = (total + brecv[:, cols(j)].astype(jnp.float32)).astype(bf16)

    if with_point:

        @pl.loop(0, tiles)
        def _(j):
            total = block(0, j)
            for d in range(1, nz):
                point_copy(d, j).wait_recv()
                total += gpr[d - 1, j].astype(jnp.float32)
            gp_ref[:, cols(j)] = total

    @pl.when(has_low)
    def _():
        to_low(0, t).wait_send()
        to_low(1, o).wait_send()
        gh_low.wait_send()

    @pl.when(has_high)
    def _():
        to_high(0, t).wait_send()
        to_high(1, o).wait_send()
        gh_high.wait_send()

    x_side.wait_send()
    d_side.wait_send()
    m_side.wait_send()
    b_side.wait_send()
    if with_point:
        d_pair.wait_send()
        d_next.wait_send()

        @pl.loop(0, tiles)
        def _(j):
            act_copy(j).wait_send()
            for d in range(1, nz):
                point_copy(d, j).wait_send()


def local(n, inputs, w_dilated, w_point, cotangent):
    T, H = inputs.shape
    C = w_point.shape[0]
    R = DILATION_BINS
    tile = 256
    tiles = H // tile
    rows = C // n
    bf16, f32 = jnp.bfloat16, jnp.float32
    with_point = rows % 16 == 0 and n % 2 == 0
    nz = n // 2
    vmem = pl.BlockSpec(memory_space=pltpu.VMEM)
    hbm = pl.BlockSpec(memory_space=pltpu.HBM)
    plane = jax.ShapeDtypeStruct((T, H), bf16)
    act_shape = (tiles, T, tile)
    outs = [plane, plane]
    scratch = []
    if with_point:
        outs += [jax.ShapeDtypeStruct((rows, H), f32)]
        scratch += [pltpu.VMEM(act_shape, bf16), pltpu.VMEM((T, C), bf16)]
    else:
        outs += [jax.ShapeDtypeStruct(act_shape, bf16), jax.ShapeDtypeStruct((T, C), bf16)]
    dma = pltpu.SemaphoreType.DMA
    scratch += [
        pltpu.VMEM((3, C, H), bf16),
        pltpu.VMEM((C, H), bf16),
        pltpu.VMEM((T + 2 * R, C), bf16),
        pltpu.VMEM((T, H), f32),
        pltpu.VMEM((T + 2 * R, H), bf16),
        pltpu.VMEM((T, H), bf16),
        pltpu.VMEM((T, H), bf16),
        pltpu.VMEM((T, H), bf16),
        pltpu.VMEM((T, H), bf16),
        dma((3 + tiles,)), dma((6,)), dma((6,)), dma((4,)), dma((4,)), dma((2,)), dma((2,)),
    ]
    if with_point:
        scratch += [
            pltpu.VMEM(act_shape, bf16),
            pltpu.VMEM((T, H), bf16),
            pltpu.VMEM((T, H), bf16),
            pltpu.VMEM((C, 2 * T), bf16),
            pltpu.VMEM((nz - 1, tiles, rows, tile), bf16),
            pltpu.VMEM((nz - 1, tiles, rows, tile), bf16),
            dma((tiles,)), dma((tiles,)), dma((nz - 1, tiles)), dma((nz - 1, tiles)),
        ]
    results = pl.pallas_call(
        functools.partial(kernel, n, tile, with_point),
        out_shape=outs,
        in_specs=[hbm] * 4,
        out_specs=[vmem] * len(outs),
        scratch_shapes=scratch,
        compiler_params=pltpu.CompilerParams(
            collective_id=0, has_side_effects=True, vmem_limit_bytes=58 * 1024 * 1024
        ),
    )(inputs, jnp.transpose(w_dilated, (1, 0, 2)), w_point, cotangent)
    if with_point:
        return tuple(results)
    output, grad_inputs, act, full_grad = results
    activation = jnp.transpose(act, (1, 0, 2)).reshape(T, H)
    grad_point = lax.psum_scatter(
        jnp.einsum("to,tc->oc", full_grad, activation, preferred_element_type=f32),
        "seq",
        scatter_dimension=0,
        tiled=True,
    )
    return (output, grad_inputs, grad_point)


def solution(mesh):
    placed = (
        P(("groups", "seq"), "tensor"),
        P(None, None, "tensor"),
        P(None, "tensor"),
        P(("groups", "seq"), "tensor"),
    )
    return jax.shard_map(
        functools.partial(local, mesh.shape["seq"]),
        mesh=mesh,
        in_specs=placed,
        out_specs=(
            P(("groups", "seq"), "tensor"),
            P(("groups", "seq"), "tensor"),
            P(("groups", "seq"), "tensor"),
        ),
        check_vma=False,
    )
```
